32 devices in a mesh: section: 4 (over z), ctx: 8 (over y, x, core).
Axes of the slice: x: 2, y: 2, z: 4, core: 2. Of those that a mesh axis runs over, the one named last changes fastest.
Arguments:
- queries: bfloat16 [4, 1024, 2048], P('section', 'ctx'), may hold values from -120 to 120
- keys_values: bfloat16 [4, 1024, 256], P('section', 'ctx'), may hold values from -6 to 6
- output: bfloat16 [4, 1024, 2048], P('section', 'ctx'), may hold values from -0.59765625 to 0.59765625
- dout: bfloat16 [4, 1024, 2048], P('section', 'ctx'), may hold values from -1.796875 to 1.796875
- segment_ids: int32 [4, 1024], P('section', 'ctx'), may hold values from 0 to 3, as said below
- span_order: int32 [16], P('ctx'), may hold values from 0 to 15, as said below
Outputs:
- upstream_query_grads: bfloat16 [4, 1024, 2048], P('section', 'ctx')
- upstream_kv_grads: bfloat16 [4, 1024, 256], P('section', 'ctx')
The draws below stay inside these ranges and needn't reach their ends.
Inputs may be any that keep to these rules, and one draw needn't show every extreme that they name: `span_order`: entries 2j and 2j + 1 are a span c below 8 and its mirror 16 - 1 - c; every span appears once. `segment_ids`: read in sequence position order, each section's document numbers never fall, and all 4 documents are present.
All inputs are finite; a program needn't handle non-finite values.
Results may differ from the reference program's by a relative error of at most 0.012.
Values may be sent and summed in bfloat16 or wider, within the bound.
A program may use at most 64 MiB of HBM per device.

```python
import jax
import jax.numpy as jnp
from jax import lax

HEAD = 128
QHEADS = 16
NDOCS = 4
SPAN = 64
SPANS = 16
SEQ = 1024
SECTIONS = 4


def attention_inputs(key):
    query_key = jax.random.fold_in(key, 101)
    pair_key = jax.random.fold_in(key, 102)
    queries = jnp.clip(jax.random.normal(query_key, (SECTIONS, SEQ, QHEADS * HEAD), jnp.float32), -6.0, 6.0)
    pairs = jnp.clip(jax.random.normal(pair_key, (SECTIONS, SEQ, 2 * HEAD), jnp.float32), -6.0, 6.0)
    return (queries, pairs)


def draw_queries(key, part):
    queries, pairs = attention_inputs(key)
    return queries.astype(jnp.bfloat16)


def draw_keys_values(key, part):
    queries, pairs = attention_inputs(key)
    return pairs.astype(jnp.bfloat16)


def span_pairs(key):
    half = SPANS // 2
    firsts = jax.random.permutation(jax.random.fold_in(key, 201), half).astype(jnp.int32)
    return jnp.stack([firsts, SPANS - 1 - firsts], axis=1).reshape(SPANS).astype(jnp.int32)


def draw_span_order(key, part):
    return span_pairs(key)


def draw_segment_ids(key, part):
    order = span_pairs(key)
    inside = jnp.tile(jnp.arange(SPAN, dtype=jnp.int32), SPANS)
    places = (jnp.repeat(order, SPAN) * SPAN + inside).astype(jnp.int32)
    section_keys = jax.random.split(jax.random.fold_in(key, 202), SECTIONS)

    def cut_points(one_key):
        return jax.random.permutation(one_key, SEQ - 1)[:NDOCS - 1].astype(jnp.int32) + 1
    cuts = jax.vmap(cut_points)(section_keys)
    positions = jnp.arange(SEQ, dtype=jnp.int32)
    in_order = jnp.sum((positions[None, :, None] >= cuts[:, None, :]).astype(jnp.int32), axis=2)
    return in_order[:, places].astype(jnp.int32)


def block_levels(own_key, shape, cuts, low, top_value):
    level, own = 1.0, jax.random.fold_in(own_key, 6)
    for position, blocks in cuts:
        draws = jnp.exp(jax.random.uniform(jax.random.fold_in(own, position), (blocks,), jnp.float32, low / len(cuts), top_value / len(cuts)))
        level = level * jnp.repeat(draws, shape[position] // blocks).reshape([-1 if axis == position else 1 for axis in range(len(shape))])
    return level


def normal_values(own_key, shape, scale, limit, cuts=(), kind=jnp.bfloat16):
    gain = block_levels(own_key, shape, cuts, -0.22, 0.18) if cuts else 1.0
    values = jax.random.normal(own_key, shape, jnp.float32) * scale * gain
    return jnp.minimum(jnp.maximum(values, -limit), limit).astype(kind)


def setup_inputs(seed: int = 0) -> dict:
    key_of = jax.random.split(jax.random.key(seed), 7)
    return {
        "queries": draw_queries(jax.random.fold_in(key_of[6], 71), 0),
        "keys_values": draw_keys_values(jax.random.fold_in(key_of[6], 71), 0),
        "output": normal_values(key_of[2], (SECTIONS, SEQ, QHEADS * HEAD), 0.1, 0.59765625, ((0, 4), (1, 8))),
        "dout": normal_values(key_of[3], (SECTIONS, SEQ, QHEADS * HEAD), 0.3, 1.796875, ((0, 4), (1, 8))),
        "segment_ids": draw_segment_ids(jax.random.fold_in(key_of[6], 71), 0),
        "span_order": draw_span_order(jax.random.fold_in(key_of[6], 71), 0),
    }


def row_places(span_order):
    inside = jnp.tile(jnp.arange(SPAN, dtype=jnp.int32), SPANS)
    return (jnp.repeat(span_order.astype(jnp.int32), SPAN) * SPAN + inside).astype(jnp.int32)


def section_grads(inputs, places):
    queries, keys_values, output, dout, segments = inputs
    scale = HEAD ** -0.5
    keys = keys_values[:, :HEAD]
    values = keys_values[:, HEAD:]
    allowed = (places[None, :] <= places[:, None]) & (segments[None, :] == segments[:, None])
    q_heads = queries.reshape(SEQ, QHEADS, HEAD).transpose(1, 0, 2)
    d_heads = dout.reshape(SEQ, QHEADS, HEAD).transpose(1, 0, 2)
    o_heads = output.reshape(SEQ, QHEADS, HEAD).transpose(1, 0, 2)

    def one_head(parts):
        q_one, d_one, o_one = parts
        scores = jnp.dot(q_one, keys.T, preferred_element_type=jnp.float32) * scale
        masked = jnp.where(allowed, scores, -jnp.inf)
        top = jnp.max(masked, axis=1, keepdims=True)
        lse = top + jnp.log(jnp.sum(jnp.exp(masked - top), axis=1, keepdims=True))
        probs = jnp.where(allowed, jnp.exp(scores - lse), 0.0)
        delta = jnp.sum(d_one.astype(jnp.float32) * o_one.astype(jnp.float32), axis=1, keepdims=True)
        d_probs = jnp.dot(d_one, values.T, preferred_element_type=jnp.float32)
        d_scores = (probs * (d_probs - delta)).astype(jnp.bfloat16)
        probs_low = probs.astype(jnp.bfloat16)
        q_grad = jnp.dot(d_scores, keys, preferred_element_type=jnp.float32) * scale
        k_grad = jnp.dot(d_scores.T, q_one, preferred_element_type=jnp.float32) * scale
        v_grad = jnp.dot(probs_low.T, d_one, preferred_element_type=jnp.float32)
        return q_grad.astype(jnp.bfloat16), jnp.concatenate([k_grad, v_grad], axis=1)

    q_grads, kv_terms = lax.map(one_head, (q_heads, d_heads, o_heads))
    q_whole = q_grads.transpose(1, 0, 2).reshape(SEQ, QHEADS * HEAD)
    kv_whole = jnp.sum(kv_terms, axis=0).astype(jnp.bfloat16)
    return q_whole, kv_whole


def reference(queries, keys_values, output, dout, segment_ids, span_order):
    places = row_places(span_order)

    def per_section(inputs):
        return section_grads(inputs, places)

    q_all, kv_all = lax.map(per_section, (queries, keys_values, output, dout, segment_ids))
    zero_q = jnp.zeros((1, SEQ, QHEADS * HEAD), jnp.bfloat16)
    zero_kv = jnp.zeros((1, SEQ, 2 * HEAD), jnp.bfloat16)
    upstream_query_grads = jnp.concatenate([q_all[1:], zero_q], axis=0)
    upstream_kv_grads = jnp.concatenate([kv_all[1:], zero_kv], axis=0)
    return upstream_query_grads, upstream_kv_grads
```

```python
import functools

import jax
import jax.numpy as jnp
from jax import lax
from jax.experimental import pallas as pl
from jax.experimental.pallas import tpu as pltpu
from jax.sharding import PartitionSpec as P

MESH = pl.DeviceIdType.MESH
NEG = -1e30
DOT = functools.partial(lax.dot_general, preferred_element_type=jnp.float32)
NT = (((1,), (1,)), ((), ()))
NN = (((1,), (0,)), ((), ()))


def kernel(
    sections, n, head, pairs, width,
    q_in, kv_in, o_in, d_in, seg_in, order_in,
    dq_out, dkv_out,
    q_s, o_s, d_s, kv_s, meta_own, meta_s, kt_s, bias_s, sc_s, p_s, ds_s, dk_s, dv_s, dq_st, rs_st, rs_in, kv_st,
    in_sem, own_sem, ag_send, ag_recv, rs_send, rs_recv, dq_send, dq_recv, kvo_send, kvo_recv,
):
    section = lax.axis_index("section")
    me = lax.axis_index("ctx")
    tok = kv_in.shape[1]
    span = tok // 2
    cols = 2 * head
    scale = head ** (-0.5)
    chunk = tok

    def loop(count, body):
        lax.fori_loop(0, count, lambda i, c: (body(i), c)[1], 0)

    def peer(i):
        return lax.rem(me + i + 1, n)

    def in_copies(g):
        at = pl.ds(pl.multiple_of(g * cols, cols), cols)
        return [
            pltpu.make_async_copy(src.at[0, :, at], dst.at[g], in_sem.at[k, g])
            for k, (src, dst) in enumerate(((q_in, q_s), (d_in, d_s), (o_in, o_s)))
        ]

    own_kv = pltpu.make_async_copy(kv_in.at[0], kv_s.at[me], own_sem)
    own_kv.start()

    barrier = pltpu.get_barrier_semaphore()

    def greet(i):
        pl.semaphore_signal(barrier, inc=1, device_id={"ctx": peer(i)}, device_id_type=MESH)

    loop(n - 1, greet)

    @pl.when(section > 0)
    def _():
        pl.semaphore_signal(barrier, inc=1, device_id={"section": section - 1}, device_id_type=MESH)

    @pl.when(section < sections - 1)
    def _():
        pl.semaphore_signal(barrier, inc=1, device_id={"section": section + 1}, device_id_type=MESH)

    loop(pairs, lambda g: [c.start() for c in in_copies(g)][0])

    lane = lax.broadcasted_iota(jnp.int32, (1, tok), 1)
    pos_row = jnp.where(lane < span, order_in[0] * span + lane, order_in[1] * span + lane - span)
    seg_row = seg_in[...]
    meta = jnp.concatenate([pos_row, seg_row, jnp.zeros((6, tok), jnp.int32)], axis=0)
    meta_own[...] = meta

    ends = (section == 0).astype(jnp.int32) + (section == sections - 1).astype(jnp.int32)
    pl.semaphore_wait(barrier, n + 1 - ends)

    def ag_copies(to, slot):
        return [
            pltpu.make_async_remote_copy(
                src, dst.at[slot], ag_send.at[k, to], ag_recv.at[k, slot],
                device_id={"ctx": to}, device_id_type=MESH,
            )
            for k, (src, dst) in enumerate(((kv_in.at[0], kv_s), (meta_own, meta_s)))
        ]

    loop(n - 1, lambda i: [c.start() for c in ag_copies(peer(i), me)][0])

    meta_s[me] = meta
    dk_s[...] = jnp.zeros_like(dk_s)
    dv_s[...] = jnp.zeros_like(dv_s)
    own_kv.wait()

    def arrive(i):
        for c in ag_copies(peer(i), peer(i)):
            c.wait_recv()

    loop(n - 1, arrive)

    pos_rows = pos_row.astype(jnp.float32)
    seg_rows = seg_row.astype(jnp.float32)

    def prepare(j):
        info = meta_s[j].astype(jnp.float32).T
        ok = (info[:, 0:1] <= pos_rows) & (info[:, 1:2] == seg_rows)
        bias_s[j] = jnp.where(ok, 0.0, NEG)
        kt_s[j] = kv_s[j, :, :head].astype(jnp.float32).T.astype(jnp.bfloat16)

    loop(n, prepare)
    loop(pairs, lambda g: [c.wait() for c in in_copies(g)][0])

    def dq_copy(g):
        at = pl.ds(pl.multiple_of(g * cols, cols), cols)
        return pltpu.make_async_remote_copy(
            dq_st.at[g], dq_out.at[0, :, at], dq_send.at[g], dq_recv.at[g],
            device_id={"section": section - 1}, device_id_type=MESH,
        )

    unroll = n <= 8

    def each(init, body):
        return lax.fori_loop(0, n, body, init, unroll=unroll)

    def pair(g):
        q2, d2, o2 = q_s[g], d_s[g], o_s[g]
        q2 = jnp.concatenate([q2[:, :head], q2[:, head:]], axis=0)
        d2 = jnp.concatenate([d2[:, :head], d2[:, head:]], axis=0)
        o2 = jnp.concatenate([o2[:, :head], o2[:, head:]], axis=0)
        delta = jnp.sum((d2.astype(jnp.float32) * o2.astype(jnp.float32)).T, axis=0, keepdims=True)

        def score(j, top):
            bias = bias_s[j]
            s = DOT(kv_s[j, :, :head], q2, NT) * scale + jnp.concatenate([bias, bias], axis=1)
            sc_s[j] = s
            return jnp.maximum(top, jnp.max(s, axis=0, keepdims=True))

        top = each(jnp.full((1, 2 * tok), NEG, jnp.float32), score)

        def expo(j, total):
            e = jnp.exp(sc_s[j] - top)
            sc_s[j] = e
            return total + jnp.sum(e, axis=0, keepdims=True)

        total = each(jnp.zeros((1, 2 * tok), jnp.float32), expo)
        inv = 1.0 / total

        def grads(j, acc):
            p = sc_s[j] * inv
            dp = DOT(kv_s[j, :, head:], d2, NT)
            ds = (p * (dp - delta)).astype(jnp.bfloat16)
            dk_s[j] += DOT(ds, q2, NN)
            dv_s[j] += DOT(p.astype(jnp.bfloat16), d2, NN)
            return acc + DOT(kt_s[j], ds, NN)

        dqt = each(jnp.zeros((head, 2 * tok), jnp.float32), grads)
        dq = (dqt * scale).T
        dq_st[g] = jnp.concatenate([dq[:tok], dq[tok:]], axis=1).astype(jnp.bfloat16)

        @pl.when(section > 0)
        def _():
            dq_copy(g).start()

    loop(pairs, pair)

    def rs_copy(to, slot):
        return pltpu.make_async_remote_copy(
            rs_st.at[to], rs_in.at[slot], rs_send.at[to], rs_recv.at[slot],
            device_id={"ctx": to}, device_id_type=MESH,
        )

    def scatter(i):
        to = peer(i)
        rs_st[to] = jnp.concatenate([dk_s[to] * scale, dv_s[to]], axis=1).astype(jnp.bfloat16)
        rs_copy(to, me).start()

    loop(n - 1, scatter)

    def gather(i, acc):
        frm = peer(i)
        rs_copy(frm, frm).wait_recv()
        return acc + rs_in[frm].astype(jnp.float32)

    own = jnp.concatenate([dk_s[me] * scale, dv_s[me]], axis=1)
    kv_st[...] = lax.fori_loop(0, n - 1, gather, own).astype(jnp.bfloat16)
    kvo = pltpu.make_async_remote_copy(
        kv_st, dkv_out.at[0], kvo_send, kvo_recv,
        device_id={"section": section - 1}, device_id_type=MESH,
    )

    @pl.when(section > 0)
    def _():
        kvo.start()

    def drain(i):
        for c in ag_copies(peer(i), me):
            c.wait_send()
        rs_copy(peer(i), me).wait_send()

    loop(n - 1, drain)

    @pl.when(section > 0)
    def _():
        loop(pairs, lambda g: dq_copy(g).wait_send())
        kvo.wait_send()

    @pl.when(section < sections - 1)
    def _():
        loop(pairs, lambda g: dq_copy(g).wait_recv())
        kvo.wait_recv()


def per_device(sections, n, queries, keys_values, output, dout, segment_ids, span_order):
    head = keys_values.shape[2] // 2
    tok, width = queries.shape[1:]
    pairs = width // (2 * head)
    cols = 2 * head
    any_spec = pl.BlockSpec(memory_space=pl.ANY)
    f32, bf16, i32 = jnp.float32, jnp.bfloat16, jnp.int32
    dma = pltpu.SemaphoreType.DMA
    dq, dkv = pl.pallas_call(
        functools.partial(kernel, sections, n, head, pairs, width),
        out_shape=(
            jax.ShapeDtypeStruct((1, tok, width), bf16),
            jax.ShapeDtypeStruct((1, tok, cols), bf16),
        ),
        in_specs=[any_spec] * 4
        + [pl.BlockSpec(memory_space=pltpu.VMEM), pl.BlockSpec(memory_space=pltpu.SMEM)],
        out_specs=(any_spec, any_spec),
        scratch_shapes=[
            pltpu.VMEM((pairs, tok, cols), bf16),
            pltpu.VMEM((pairs, tok, cols), bf16),
            pltpu.VMEM((pairs, tok, cols), bf16),
            pltpu.VMEM((n, tok, cols), bf16),
            pltpu.VMEM((8, tok), i32),
            pltpu.VMEM((n, 8, tok), i32),
            pltpu.VMEM((n, head, tok), bf16),
            pltpu.VMEM((n, tok, tok), f32),
            pltpu.VMEM((n, tok, 2 * tok), f32),
            pltpu.VMEM((8, 128), f32),
            pltpu.VMEM((8, 128), f32),
            pltpu.VMEM((n, tok, head), f32),
            pltpu.VMEM((n, tok, head), f32),
            pltpu.VMEM((pairs, tok, cols), bf16),
            pltpu.VMEM((n, tok, cols), bf16),
            pltpu.VMEM((n, tok, cols), bf16),
            pltpu.VMEM((tok, cols), bf16),
            dma((3, pairs)),
            dma,
            dma((2, n)),
            dma((2, n)),
            dma((n,)),
            dma((n,)),
            dma((pairs,)),
            dma((pairs,)),
            dma,
            dma,
        ],
        compiler_params=pltpu.CompilerParams(
            collective_id=0, has_side_effects=True, vmem_limit_bytes=48 << 20
        ),
    )(queries, keys_values, output, dout, segment_ids, span_order)
    last = lax.axis_index("section") == sections - 1
    return (
        jnp.where(last, jnp.zeros_like(dq), dq),
        jnp.where(last, jnp.zeros_like(dkv), dkv),
    )


def solution(mesh):
    rows = P("section", "ctx", None)
    return jax.shard_map(
        functools.partial(per_device, mesh.shape["section"], mesh.shape["ctx"]),
        mesh=mesh,
        in_specs=(rows, rows, rows, rows, P("section", "ctx"), P("ctx")),
        out_specs=(rows, rows),
        check_vma=False,
    )
```

```python
import functools

import jax
import jax.numpy as jnp
from jax import lax
from jax.experimental import pallas as pl
from jax.experimental.pallas import tpu as pltpu
from jax.sharding import PartitionSpec as P

MESH = pl.DeviceIdType.MESH
NEG = -1e30
DOT = functools.partial(lax.dot_general, preferred_element_type=jnp.float32)
NT = (((1,), (1,)), ((), ()))
NN = (((1,), (0,)), ((), ()))


def kernel(
    sections, n, head, heads,
    q_in, kv_in, o_in, d_in, seg_in, order_in,
    dq_out, dkv_out,
    q_s, o_s, d_s, kv_s, seg_s, meta_own, meta_s, flag_v, flag_m, k_a, k_b, kt_a, kt_b, bias_a, bias_b,
    sc_a, sc_b, ds_a, ds_be, ds_bl, dka_s, dva_s, dkb_s, dvb_s, dq_st, rs_st, rs_in, kv_st,
    in_sem, own_sem, seg_sem, flag_sem, ag_send, ag_recv, rs_send, rs_recv, dq_send, dq_recv, kvo_send, kvo_recv,
):
    section = lax.axis_index("section")
    me = lax.axis_index("ctx")
    tok = kv_in.shape[1]
    span = tok // 2
    cols = 2 * head
    scale = head ** (-0.5)

    def loop(count, body):
        lax.fori_loop(0, count, lambda i, c: (body(i), c)[1], 0)

    def peer(i):
        return lax.rem(me + i + 1, n)

    quad = 4
    quads = heads // quad
    wide = quad * span

    def in_copies(i):
        g, half, h = i // (2 * quad), lax.rem(i // quad, 2), lax.rem(i, quad)
        at = pl.ds(pl.multiple_of((g * quad + h) * head, head), head)
        rows = pl.ds(pl.multiple_of(half * span, span), span)
        to = pl.ds(pl.multiple_of(h * span, span), span)
        return [
            pltpu.make_async_copy(src.at[0, rows, at], dst.at[g, half, to], in_sem.at[k, i])
            for k, (src, dst) in enumerate(((q_in, q_s), (d_in, d_s), (o_in, o_s)))
        ]

    own_kv = pltpu.make_async_copy(kv_in.at[0], kv_s.at[me], own_sem)
    own_kv.start()
    own_seg = pltpu.make_async_copy(seg_in, seg_s, seg_sem)
    own_seg.start()

    barrier = pltpu.get_barrier_semaphore()

    def greet(i):
        pl.semaphore_signal(barrier, inc=1, device_id={"ctx": peer(i)}, device_id_type=MESH)

    loop(n - 1, greet)

    @pl.when(section > 0)
    def _():
        pl.semaphore_signal(barrier, inc=1, device_id={"section": section - 1}, device_id_type=MESH)

    @pl.when(section < sections - 1)
    def _():
        pl.semaphore_signal(barrier, inc=1, device_id={"section": section + 1}, device_id_type=MESH)

    loop(2 * heads, lambda g: [c.start() for c in in_copies(g)][0])

    lane = lax.broadcasted_iota(jnp.int32, (1, tok), 1)
    pos_row = jnp.where(lane < span, order_in[0] * span + lane, order_in[1] * span + lane - span)
    own_seg.wait()
    seg_row = seg_s[...]
    meta = jnp.concatenate([pos_row, seg_row, jnp.full((6, tok), order_in[0], jnp.int32)], axis=0)
    meta_own[...] = meta

    ends = (section == 0).astype(jnp.int32) + (section == sections - 1).astype(jnp.int32)
    pl.semaphore_wait(barrier, n + 1 - ends)

    def ag_copies(to, slot):
        return [
            pltpu.make_async_remote_copy(
                src, dst.at[slot], ag_send.at[k, to], ag_recv.at[k, slot],
                device_id={"ctx": to}, device_id_type=MESH,
            )
            for k, (src, dst) in enumerate(((kv_in.at[0], kv_s), (meta_own, meta_s)))
        ]

    loop(n - 1, lambda i: [c.start() for c in ag_copies(peer(i), me)][0])

    meta_s[me] = meta
    for acc in (dka_s, dva_s, dkb_s, dvb_s):
        acc[...] = jnp.zeros_like(acc)
    ds_a[(n + 1) * span :] = jnp.zeros((span, wide), jnp.bfloat16)
    kt_a[:, n * span :] = jnp.zeros((head, 2 * span), jnp.bfloat16)

    inside = jnp.where(lane < span, lane, lane - span)
    pos_e = (order_in[0] * span + inside).astype(jnp.float32)
    pos_l = (order_in[1] * span + inside).astype(jnp.float32)
    seg_f = seg_row.astype(jnp.float32)
    seg_r = pltpu.roll(seg_f, span, 1)
    seg_e = jnp.where(lane < span, seg_f, seg_r)
    seg_l = jnp.where(lane < span, seg_r, seg_f)

    def bias_of(key, pos, seg):
        ok = (key[:, 0:1] <= pos) & (key[:, 1:2] == seg)
        return jnp.where(ok, 0.0, NEG)

    def block(j):
        return pl.ds(pl.multiple_of(j * span, span), span)

    def prepare(j):
        got = meta_s[j]
        info = got.astype(jnp.float32).T
        kv = kv_s[j].astype(jnp.float32)
        flag = got[2:3] <= order_in[0]
        flag_v[pl.ds(j, 1)] = flag.astype(jnp.int32)
        bias_a[block(j)] = bias_of(info[:span], pos_l, seg_l)
        k_a[block(j)] = kv_s[j, :span]
        kind = jnp.where(flag, 1.0, 0.0)
        lanes2 = jnp.concatenate([kind, kind], axis=1)
        kv_b = jnp.where(lanes2 > 0.5, kv[:span], kv[span:])
        k_b[block(j)] = kv_b.astype(jnp.bfloat16)
        info_b = jnp.where(kind[:, :8] > 0.5, info[:span], info[span:])
        bias_b[block(j)] = bias_of(
            info_b, jnp.where(flag, pos_e, pos_l), jnp.where(flag, seg_e, seg_l)
        )

        @pl.when(j == me)
        def _():
            last = pl.ds(n * span, span)
            k_a[last] = kv_s[j, span:]
            bias_a[last] = bias_of(info[span:], pos_l, seg_l)

    own_kv.wait()
    prepare(me)

    def arrive(i):
        for c in ag_copies(peer(i), peer(i)):
            c.wait_recv()
        prepare(peer(i))

    loop(n - 1, arrive)
    flags = pltpu.make_async_copy(flag_v, flag_m, flag_sem)
    flags.start()

    def turn(j):
        at = pl.ds(pl.multiple_of(j * tok, tok), tok)
        rows = pl.ds(pl.multiple_of(j * tok, tok), tok)
        kt_a[:, at] = k_a[rows, :head].astype(jnp.float32).T.astype(jnp.bfloat16)
        kt_b[:, at] = k_b[rows, :head].astype(jnp.float32).T.astype(jnp.bfloat16)

    loop(n // 2, turn)
    kt_a[:, pl.ds(n * span, tok)] = jnp.concatenate(
        [k_a[pl.ds(n * span, span), :head].astype(jnp.float32).T, jnp.zeros((head, span), jnp.float32)],
        axis=1,
    ).astype(jnp.bfloat16)
    loop(2 * heads, lambda g: [c.wait() for c in in_copies(g)][0])
    flags.wait()

    def dq_copy(g):
        at = pl.ds(pl.multiple_of(g * quad * head, quad * head), quad * head)
        return pltpu.make_async_remote_copy(
            dq_st.at[g], dq_out.at[0, :, at], dq_send.at[g], dq_recv.at[g],
            device_id={"section": section - 1}, device_id_type=MESH,
        )

    size = max(d for d in range(1, 17) if (n + 1) % d == 0)
    steps = (n + 1) // size
    size *= span

    def each(count, init, body):
        return lax.fori_loop(0, count, body, init, unroll=count <= 8)

    def part(c):
        return pl.ds(pl.multiple_of(c * size, span), size)

    def twice(x):
        return jnp.concatenate([x, x], axis=1)

    def group(g):
        q_l, d_l = q_s[g, 1], d_s[g, 1]

        def delta_of(half):
            prod = d_s[g, half].astype(jnp.float32) * o_s[g, half].astype(jnp.float32)
            return jnp.sum(prod.T, axis=0, keepdims=True)

        delta_e, delta_l = delta_of(0), delta_of(1)

        def flag_of(j):
            return flag_m[j, 0]

        def choose(f, early, late):
            return jnp.where(f > 0, early, late)

        low = jnp.full((1, wide), NEG, jnp.float32)
        none = jnp.zeros((1, wide), jnp.float32)

        def score_a(c, top):
            s = DOT(k_a[part(c), :head], q_l, NT) * scale + twice(bias_a[part(c)])
            sc_a[part(c)] = s
            return jnp.maximum(top, jnp.max(s, axis=0, keepdims=True))

        def score_b(j, tops):
            f = flag_of(j)
            s = DOT(k_b[block(j), :head], q_s[g, 1 - f], NT) * scale + twice(bias_b[block(j)])
            sc_b[block(j)] = s
            top = jnp.max(s, axis=0, keepdims=True)
            return (
                jnp.maximum(tops[0], choose(f, top, low)),
                jnp.maximum(tops[1], choose(f, low, top)),
            )

        top_e, top_l = each(n, (low, each(steps, low, score_a)), score_b)

        def exp_a(c, total):
            e = jnp.exp(sc_a[part(c)] - top_l)
            sc_a[part(c)] = e
            return total + jnp.sum(e, axis=0, keepdims=True)

        def exp_b(j, totals):
            f = flag_of(j)
            e = jnp.exp(sc_b[block(j)] - choose(f, top_e, top_l))
            sc_b[block(j)] = e
            total = jnp.sum(e, axis=0, keepdims=True)
            return (totals[0] + choose(f, total, none), totals[1] + choose(f, none, total))

        total_e, total_l = each(n, (none, each(steps, none, exp_a)), exp_b)
        inv_e, inv_l = 1.0 / total_e, 1.0 / total_l

        def grads_a(c, unused):
            p = sc_a[part(c)] * inv_l
            dp = DOT(k_a[part(c), head:], d_l, NT)
            ds = (p * (dp - delta_l)).astype(jnp.bfloat16)
            ds_a[part(c)] = ds
            dka_s[part(c)] += DOT(ds, q_l, NN)
            dva_s[part(c)] += DOT(p.astype(jnp.bfloat16), d_l, NN)
            return unused

        def grads_b(j, unused):
            f = flag_of(j)
            q_j, d_j = q_s[g, 1 - f], d_s[g, 1 - f]
            p = sc_b[block(j)] * choose(f, inv_e, inv_l)
            dp = DOT(k_b[block(j), head:], d_j, NT)
            ds = p * (dp - choose(f, delta_e, delta_l))
            ds_e = ds * f.astype(jnp.float32)
            ds_be[block(j)] = ds_e.astype(jnp.bfloat16)
            ds_bl[block(j)] = (ds - ds_e).astype(jnp.bfloat16)
            dkb_s[block(j)] += DOT(ds.astype(jnp.bfloat16), q_j, NN)
            dvb_s[block(j)] += DOT(p.astype(jnp.bfloat16), d_j, NN)
            return unused

        each(steps, 0, grads_a)
        each(n, 0, grads_b)
        dq_l = (DOT(kt_a[...], ds_a[...], NN) + DOT(kt_b[...], ds_bl[...], NN)) * scale
        dq_e = DOT(kt_b[...], ds_be[...], NN) * scale
        for half, dqt in ((0, dq_e), (1, dq_l)):
            dq = dqt.T.astype(jnp.bfloat16)
            dq_st[g, half * span : (half + 1) * span] = jnp.concatenate(
                [dq[h * span : (h + 1) * span] for h in range(quad)], axis=1
            )

        @pl.when(section > 0)
        def _():
            dq_copy(g).start()

    loop(quads, group)

    def terms(j):
        f = flag_m[j, 0].astype(jnp.float32)
        dk_b, dv_b = dkb_s[block(j)], dvb_s[block(j)]
        dk_e, dv_e = dk_b * f, dv_b * f
        return jnp.concatenate(
            [
                jnp.concatenate([(dka_s[block(j)] + dk_e) * scale, dva_s[block(j)] + dv_e], axis=1),
                jnp.concatenate([(dk_b - dk_e) * scale, dv_b - dv_e], axis=1),
            ],
            axis=0,
        )

    def rs_copy(to, slot):
        return pltpu.make_async_remote_copy(
            rs_st.at[to], rs_in.at[slot], rs_send.at[to], rs_recv.at[slot],
            device_id={"ctx": to}, device_id_type=MESH,
        )

    def scatter(i):
        to = peer(i)
        rs_st[to] = terms(to).astype(jnp.bfloat16)
        rs_copy(to, me).start()

    loop(n - 1, scatter)

    def gather(i, acc):
        frm = peer(i)
        rs_copy(frm, frm).wait_recv()
        return acc + rs_in[frm].astype(jnp.float32)

    last = pl.ds(n * span, span)
    diag = jnp.concatenate([dka_s[last] * scale, dva_s[last]], axis=1)
    own = terms(me) + jnp.concatenate([jnp.zeros_like(diag), diag], axis=0)
    kv_st[...] = lax.fori_loop(0, n - 1, gather, own).astype(jnp.bfloat16)
    kvo = pltpu.make_async_remote_copy(
        kv_st, dkv_out.at[0], kvo_send, kvo_recv,
        device_id={"section": section - 1}, device_id_type=MESH,
    )

    @pl.when(section > 0)
    def _():
        kvo.start()

    def drain(i):
        for c in ag_copies(peer(i), me):
            c.wait_send()
        rs_copy(peer(i), me).wait_send()

    loop(n - 1, drain)

    @pl.when(section > 0)
    def _():
        loop(quads, lambda g: dq_copy(g).wait_send())
        kvo.wait_send()

    @pl.when(section < sections - 1)
    def _():
        loop(quads, lambda g: dq_copy(g).wait_recv())
        kvo.wait_recv()


def per_device(sections, n, queries, keys_values, output, dout, segment_ids, span_order):
    head = keys_values.shape[2] // 2
    tok, width = queries.shape[1:]
    heads = width // head
    quads = heads // 4
    span = tok // 2
    wide = 4 * span
    cols = 2 * head
    in_a, in_b = (n + 1) * span, n * span
    any_spec = pl.BlockSpec(memory_space=pl.ANY)
    hbm_spec = pl.BlockSpec(memory_space=pltpu.HBM)
    f32, bf16, i32 = jnp.float32, jnp.bfloat16, jnp.int32
    dma = pltpu.SemaphoreType.DMA
    dq, dkv = pl.pallas_call(
        functools.partial(kernel, sections, n, head, heads),
        out_shape=(
            jax.ShapeDtypeStruct((1, tok, width), bf16),
            jax.ShapeDtypeStruct((1, tok, cols), bf16),
        ),
        in_specs=[hbm_spec] * 5 + [pl.BlockSpec(memory_space=pltpu.SMEM)],
        out_specs=(any_spec, any_spec),
        scratch_shapes=[
            pltpu.VMEM((quads, 2, wide, head), bf16),
            pltpu.VMEM((quads, 2, wide, head), bf16),
            pltpu.VMEM((quads, 2, wide, head), bf16),
            pltpu.VMEM((n, tok, cols), bf16),
            pltpu.VMEM((1, tok), i32),
            pltpu.VMEM((8, tok), i32),
            pltpu.VMEM((n, 8, tok), i32),
            pltpu.VMEM((n, tok), i32),
            pltpu.SMEM((n, tok), i32),
            pltpu.VMEM((in_a, cols), bf16),
            pltpu.VMEM((in_b, cols), bf16),
            pltpu.VMEM((head, in_a + span), bf16),
            pltpu.VMEM((head, in_b), bf16),
            pltpu.VMEM((in_a, tok), f32),
            pltpu.VMEM((in_b, tok), f32),
            pltpu.VMEM((in_a, wide), f32),
            pltpu.VMEM((in_b, wide), f32),
            pltpu.VMEM((in_a + span, wide), bf16),
            pltpu.VMEM((in_b, wide), bf16),
            pltpu.VMEM((in_b, wide), bf16),
            pltpu.VMEM((in_a, head), f32),
            pltpu.VMEM((in_a, head), f32),
            pltpu.VMEM((in_b, head), f32),
            pltpu.VMEM((in_b, head), f32),
            pltpu.VMEM((quads, tok, 4 * head), bf16),
            pltpu.VMEM((n, tok, cols), bf16),
            pltpu.VMEM((n, tok, cols), bf16),
            pltpu.VMEM((tok, cols), bf16),
            dma((3, 2 * heads)),
            dma,
            dma,
            dma,
            dma((2, n)),
            dma((2, n)),
            dma((n,)),
            dma((n,)),
            dma((quads,)),
            dma((quads,)),
            dma,
            dma,
        ],
        compiler_params=pltpu.CompilerParams(
            collective_id=0, has_side_effects=True, vmem_limit_bytes=60 << 20
        ),
    )(queries, keys_values, output, dout, segment_ids, span_order)
    last = lax.axis_index("section") == sections - 1
    return (
        jnp.where(last, jnp.zeros_like(dq), dq),
        jnp.where(last, jnp.zeros_like(dkv), dkv),
    )


def solution(mesh):
    rows = P("section", "ctx", None)
    return jax.shard_map(
        functools.partial(per_device, mesh.shape["section"], mesh.shape["ctx"]),
        mesh=mesh,
        in_specs=(rows, rows, rows, rows, P("section", "ctx"), P("ctx")),
        out_specs=(rows, rows),
        check_vma=False,
    )
```

```python
import functools

import jax
import jax.numpy as jnp
from jax import lax
from jax.experimental import pallas as pl
from jax.experimental.pallas import tpu as pltpu
from jax.sharding import PartitionSpec as P

MESH = pl.DeviceIdType.MESH
NEG = -1e30
DOT = functools.partial(lax.dot_general, preferred_element_type=jnp.float32)
NT = (((1,), (1,)), ((), ()))
NN = (((1,), (0,)), ((), ()))


def kernel(
    sections, n, head, heads,
    q_in, kv_in, o_in, d_in, seg_in, order_in,
    dq_out, dkv_out,
    q_s, o_s, d_s, kv_s, seg_s, meta_own, meta_s, flag_v, flag_m, k_a, k_b, kt_a, kt_b, bias_a, bias_b,
    sc_a, sc_b, ds_a, ds_be, ds_bl, dka_s, dva_s, dkb_s, dvb_s, dq_st, rs_st, rs_mid, rs_in, rs_own, kv_st,
    in_sem, own_sem, seg_sem, flag_sem, ag_send, ag_recv, rs_send, mid_recv, rs_recv, dq_send, dq_recv, kvo_send, kvo_recv,
):
    section = lax.axis_index("section")
    me = lax.axis_index("ctx")
    tok = kv_in.shape[1]
    span = tok // 2
    cols = 2 * head
    scale = head ** (-0.5)

    def loop(count, body):
        lax.fori_loop(0, count, lambda i, c: (body(i), c)[1], 0)

    chips = n // 2
    chip, core = me // 2, lax.rem(me, 2)
    partner = me + 1 - 2 * core

    def same(i):
        return 2 * lax.rem(chip + i + 1, chips) + core

    def other(i):
        return 2 * lax.rem(chip + i + 1, chips) + 1 - core

    quad = 4
    quads = heads // quad
    wide = quad * span

    def in_copies(i):
        g, half, h = i // (2 * quad), lax.rem(i // quad, 2), lax.rem(i, quad)
        at = pl.ds(pl.multiple_of((g * quad + h) * head, head), head)
        rows = pl.ds(pl.multiple_of(half * span, span), span)
        to = pl.ds(pl.multiple_of(h * span, span), span)
        return [
            pltpu.make_async_copy(src.at[0, rows, at], dst.at[g, half, to], in_sem.at[k, i])
            for k, (src, dst) in enumerate(((q_in, q_s), (d_in, d_s), (o_in, o_s)))
        ]

    own_kv = pltpu.make_async_copy(kv_in.at[0], kv_s.at[me], own_sem)
    own_kv.start()
    own_seg = pltpu.make_async_copy(seg_in, seg_s, seg_sem)
    own_seg.start()

    barrier = pltpu.get_barrier_semaphore()

    def greet(to):
        pl.semaphore_signal(barrier, inc=1, device_id={"ctx": to}, device_id_type=MESH)

    loop(chips - 1, lambda i: greet(same(i)))
    greet(partner)

    @pl.when(section > 0)
    def _():
        pl.semaphore_signal(barrier, inc=1, device_id={"section": section - 1}, device_id_type=MESH)

    @pl.when(section < sections - 1)
    def _():
        pl.semaphore_signal(barrier, inc=1, device_id={"section": section + 1}, device_id_type=MESH)

    loop(2 * heads, lambda g: [c.start() for c in in_copies(g)][0])

    lane = lax.broadcasted_iota(jnp.int32, (1, tok), 1)
    pos_row = jnp.where(lane < span, order_in[0] * span + lane, order_in[1] * span + lane - span)
    own_seg.wait()
    seg_row = seg_s[...]
    meta = jnp.concatenate([pos_row, seg_row, jnp.full((6, tok), order_in[0], jnp.int32)], axis=0)
    meta_own[...] = meta

    ends = (section == 0).astype(jnp.int32) + (section == sections - 1).astype(jnp.int32)
    pl.semaphore_wait(barrier, chips + 2 - ends)

    def ag_copies(to, slot, kv, info, via):
        return [
            pltpu.make_async_remote_copy(
                src, dst.at[slot], ag_send.at[k, via], ag_recv.at[k, slot],
                device_id={"ctx": to}, device_id_type=MESH,
            )
            for k, (src, dst) in enumerate(((info, meta_s), (kv, kv_s)))
        ]

    def ag_own(to):
        return ag_copies(to, me, kv_in.at[0], meta_own, to)

    def ag_relay(i):
        return ag_copies(partner, same(i), kv_s.at[same(i)], meta_s.at[same(i)], other(i))

    def start(copies):
        for c in copies:
            c.start()

    def arrived(frm):
        for c in ag_copies(partner, frm, kv_s.at[frm], meta_s.at[frm], frm):
            c.wait_recv()

    loop(chips - 1, lambda i: start(ag_own(same(i))))
    start(ag_own(partner))

    meta_s[me] = meta
    for acc in (dka_s, dva_s, dkb_s, dvb_s):
        acc[...] = jnp.zeros_like(acc)
    ds_a[(n + 1) * span :] = jnp.zeros((span, wide), jnp.bfloat16)
    kt_a[:, n * span :] = jnp.zeros((head, 2 * span), jnp.bfloat16)

    inside = jnp.where(lane < span, lane, lane - span)
    pos_e = (order_in[0] * span + inside).astype(jnp.float32)
    pos_l = (order_in[1] * span + inside).astype(jnp.float32)
    seg_f = seg_row.astype(jnp.float32)
    seg_r = pltpu.roll(seg_f, span, 1)
    seg_e = jnp.where(lane < span, seg_f, seg_r)
    seg_l = jnp.where(lane < span, seg_r, seg_f)

    def bias_of(key, pos, seg):
        ok = (key[:, 0:1] <= pos) & (key[:, 1:2] == seg)
        return jnp.where(ok, 0.0, NEG)

    def block(j):
        return pl.ds(pl.multiple_of(j * span, span), span)

    def prepare(j):
        got = meta_s[j]
        info = got.astype(jnp.float32).T
        kv = kv_s[j].astype(jnp.float32)
        flag = got[2:3] <= order_in[0]
        flag_v[pl.ds(j, 1)] = flag.astype(jnp.int32)
        bias_a[block(j)] = bias_of(info[:span], pos_l, seg_l)
        k_a[block(j)] = kv_s[j, :span]
        kind = jnp.where(flag, 1.0, 0.0)
        lanes2 = jnp.concatenate([kind, kind], axis=1)
        kv_b = jnp.where(lanes2 > 0.5, kv[:span], kv[span:])
        k_b[block(j)] = kv_b.astype(jnp.bfloat16)
        info_b = jnp.where(kind[:, :8] > 0.5, info[:span], info[span:])
        bias_b[block(j)] = bias_of(
            info_b, jnp.where(flag, pos_e, pos_l), jnp.where(flag, seg_e, seg_l)
        )

        @pl.when(j == me)
        def _():
            last = pl.ds(n * span, span)
            k_a[last] = kv_s[j, span:]
            bias_a[last] = bias_of(info[span:], pos_l, seg_l)

    own_kv.wait()
    prepare(me)

    arrived(partner)
    prepare(partner)

    def relay(i):
        arrived(same(i))
        start(ag_relay(i))
        prepare(same(i))

    loop(chips - 1, relay)

    def arrive(i):
        arrived(other(i))
        prepare(other(i))

    loop(chips - 1, arrive)
    flags = pltpu.make_async_copy(flag_v, flag_m, flag_sem)
    flags.start()

    def turn(j):
        at = pl.ds(pl.multiple_of(j * tok, tok), tok)
        rows = pl.ds(pl.multiple_of(j * tok, tok), tok)
        kt_a[:, at] = k_a[rows, :head].astype(jnp.float32).T.astype(jnp.bfloat16)
        kt_b[:, at] = k_b[rows, :head].astype(jnp.float32).T.astype(jnp.bfloat16)

    lax.fori_loop(0, n // 2, lambda j, c: (turn(j), c)[1], 0, unroll=n <= 8)
    kt_a[:, pl.ds(n * span, tok)] = jnp.concatenate(
        [k_a[pl.ds(n * span, span), :head].astype(jnp.float32).T, jnp.zeros((head, span), jnp.float32)],
        axis=1,
    ).astype(jnp.bfloat16)
    loop(2 * heads, lambda g: [c.wait() for c in in_copies(g)][0])
    flags.wait()

    def dq_copy(g):
        at = pl.ds(pl.multiple_of(g * quad * head, quad * head), quad * head)
        return pltpu.make_async_remote_copy(
            dq_st.at[g], dq_out.at[0, :, at], dq_send.at[g], dq_recv.at[g],
            device_id={"section": section - 1}, device_id_type=MESH,
        )

    size = max(d for d in range(1, 17) if (n + 1) % d == 0)
    steps = (n + 1) // size
    size *= span

    def each(count, init, body):
        return lax.fori_loop(0, count, body, init, unroll=count <= 8)

    def part(c):
        return pl.ds(pl.multiple_of(c * size, span), size)

    def twice(x):
        return jnp.concatenate([x, x], axis=1)

    def group(g):
        q_l, d_l = q_s[g, 1], d_s[g, 1]

        def delta_of(half):
            prod = d_s[g, half].astype(jnp.float32) * o_s[g, half].astype(jnp.float32)
            return jnp.sum(prod.T, axis=0, keepdims=True)

        delta_e, delta_l = delta_of(0), delta_of(1)

        def flag_of(j):
            return flag_m[j, 0]

        def choose(f, early, late):
            return jnp.where(f > 0, early, late)

        low = jnp.full((1, wide), NEG, jnp.float32)
        none = jnp.zeros((1, wide), jnp.float32)

        def score_a(c, top):
            s = DOT(k_a[part(c), :head], q_l, NT) * scale + twice(bias_a[part(c)])
            sc_a[part(c)] = s
            return jnp.maximum(top, jnp.max(s, axis=0, keepdims=True))

        def score_b(j, tops):
            f = flag_of(j)
            s = DOT(k_b[block(j), :head], q_s[g, 1 - f], NT) * scale + twice(bias_b[block(j)])
            sc_b[block(j)] = s
            top = jnp.max(s, axis=0, keepdims=True)
            return (
                jnp.maximum(tops[0], choose(f, top, low)),
                jnp.maximum(tops[1], choose(f, low, top)),
            )

        top_e, top_l = each(n, (low, each(steps, low, score_a)), score_b)

        def exp_a(c, total):
            e = jnp.exp(sc_a[part(c)] - top_l)
            sc_a[part(c)] = e
            return total + jnp.sum(e, axis=0, keepdims=True)

        def exp_b(j, totals):
            f = flag_of(j)
            e = jnp.exp(sc_b[block(j)] - choose(f, top_e, top_l))
            sc_b[block(j)] = e
            total = jnp.sum(e, axis=0, keepdims=True)
            return (totals[0] + choose(f, total, none), totals[1] + choose(f, none, total))

        total_e, total_l = each(n, (none, each(steps, none, exp_a)), exp_b)
        inv_e, inv_l = 1.0 / total_e, 1.0 / total_l

        def grads_a(c, unused):
            p = sc_a[part(c)] * inv_l
            dp = DOT(k_a[part(c), head:], d_l, NT)
            ds = (p * (dp - delta_l)).astype(jnp.bfloat16)
            ds_a[part(c)] = ds
            dka_s[part(c)] += DOT(ds, q_l, NN)
            dva_s[part(c)] += DOT(p.astype(jnp.bfloat16), d_l, NN)
            return unused

        def grads_b(j, unused):
            f = flag_of(j)
            q_j, d_j = q_s[g, 1 - f], d_s[g, 1 - f]
            p = sc_b[block(j)] * choose(f, inv_e, inv_l)
            dp = DOT(k_b[block(j), head:], d_j, NT)
            ds = p * (dp - choose(f, delta_e, delta_l))
            ds_e = ds * f.astype(jnp.float32)
            ds_be[block(j)] = ds_e.astype(jnp.bfloat16)
            ds_bl[block(j)] = (ds - ds_e).astype(jnp.bfloat16)
            dkb_s[block(j)] += DOT(ds.astype(jnp.bfloat16), q_j, NN)
            dvb_s[block(j)] += DOT(p.astype(jnp.bfloat16), d_j, NN)
            return unused

        each(steps, 0, grads_a)
        each(n, 0, grads_b)
        dq_l = (DOT(kt_a[...], ds_a[...], NN) + DOT(kt_b[...], ds_bl[...], NN)) * scale
        dq_e = DOT(kt_b[...], ds_be[...], NN) * scale
        for half, dqt in ((0, dq_e), (1, dq_l)):
            dq = dqt.T.astype(jnp.bfloat16)
            dq_st[g, half * span : (half + 1) * span] = jnp.concatenate(
                [dq[h * span : (h + 1) * span] for h in range(quad)], axis=1
            )

        @pl.when(section > 0)
        def _():
            dq_copy(g).start()

    loop(quads, group)

    def terms(j):
        f = flag_m[j, 0].astype(jnp.float32)
        dk_b, dv_b = dkb_s[block(j)], dvb_s[block(j)]
        dk_e, dv_e = dk_b * f, dv_b * f
        return jnp.concatenate(
            [
                jnp.concatenate([(dka_s[block(j)] + dk_e) * scale, dva_s[block(j)] + dv_e], axis=1),
                jnp.concatenate([(dk_b - dk_e) * scale, dv_b - dv_e], axis=1),
            ],
            axis=0,
        )

    def mid_copy(q):
        return pltpu.make_async_remote_copy(
            rs_st.at[2 * q + 1 - core], rs_mid.at[q], rs_send.at[2 * q + 1 - core], mid_recv.at[q],
            device_id={"ctx": partner}, device_id_type=MESH,
        )

    def rs_copy(to, slot):
        return pltpu.make_async_remote_copy(
            rs_st.at[to], rs_in.at[slot], rs_send.at[to], rs_recv.at[slot],
            device_id={"ctx": to}, device_id_type=MESH,
        )

    def hand(i):
        q = lax.rem(chip + i + 1, chips)
        rs_st[2 * q + 1 - core] = terms(2 * q + 1 - core).astype(jnp.bfloat16)
        mid_copy(q).start()

    loop(chips, hand)

    def scatter(i):
        to = same(i)
        mid_copy(to // 2).wait_recv()
        rs_st[to] = (terms(to) + rs_mid[to // 2].astype(jnp.float32)).astype(jnp.bfloat16)
        rs_copy(to, chip).start()

    loop(chips - 1, scatter)

    last = pl.ds(n * span, span)
    diag = jnp.concatenate([dka_s[last] * scale, dva_s[last]], axis=1)
    mid_copy(chip).wait_recv()
    own = terms(me) + jnp.concatenate([jnp.zeros_like(diag), diag], axis=0)
    rs_own[...] = own + rs_mid[chip].astype(jnp.float32)

    def gather(i):
        q = lax.rem(chip + i + 1, chips)
        rs_copy(same(i), q).wait_recv()
        rs_own[...] += rs_in[q].astype(jnp.float32)

    loop(chips - 1, gather)
    kv_st[...] = rs_own[...].astype(jnp.bfloat16)
    kvo = pltpu.make_async_remote_copy(
        kv_st, dkv_out.at[0], kvo_send, kvo_recv,
        device_id={"section": section - 1}, device_id_type=MESH,
    )

    @pl.when(section > 0)
    def _():
        kvo.start()

    def sent(copies):
        for c in copies:
            c.wait_send()

    def drain(i):
        sent(ag_own(same(i)))
        sent(ag_relay(i))
        rs_copy(same(i), chip).wait_send()

    loop(chips - 1, drain)
    sent(ag_own(partner))
    loop(chips, lambda q: mid_copy(q).wait_send())

    @pl.when(section > 0)
    def _():
        loop(quads, lambda g: dq_copy(g).wait_send())
        kvo.wait_send()

    @pl.when(section < sections - 1)
    def _():
        loop(quads, lambda g: dq_copy(g).wait_recv())
        kvo.wait_recv()


def per_device(sections, n, queries, keys_values, output, dout, segment_ids, span_order):
    head = keys_values.shape[2] // 2
    tok, width = queries.shape[1:]
    heads = width // head
    quads = heads // 4
    span = tok // 2
    wide = 4 * span
    cols = 2 * head
    in_a, in_b = (n + 1) * span, n * span
    any_spec = pl.BlockSpec(memory_space=pl.ANY)
    hbm_spec = pl.BlockSpec(memory_space=pltpu.HBM)
    f32, bf16, i32 = jnp.float32, jnp.bfloat16, jnp.int32
    dma = pltpu.SemaphoreType.DMA
    dq, dkv = pl.pallas_call(
        functools.partial(kernel, sections, n, head, heads),
        out_shape=(
            jax.ShapeDtypeStruct((1, tok, width), bf16),
            jax.ShapeDtypeStruct((1, tok, cols), bf16),
        ),
        in_specs=[hbm_spec] * 5 + [pl.BlockSpec(memory_space=pltpu.SMEM)],
        out_specs=(any_spec, any_spec),
        scratch_shapes=[
            pltpu.VMEM((quads, 2, wide, head), bf16),
            pltpu.VMEM((quads, 2, wide, head), bf16),
            pltpu.VMEM((quads, 2, wide, head), bf16),
            pltpu.VMEM((n, tok, cols), bf16),
            pltpu.VMEM((1, tok), i32),
            pltpu.VMEM((8, tok), i32),
            pltpu.VMEM((n, 8, tok), i32),
            pltpu.VMEM((n, tok), i32),
            pltpu.SMEM((n, tok), i32),
            pltpu.VMEM((in_a, cols), bf16),
            pltpu.VMEM((in_b, cols), bf16),
            pltpu.VMEM((head, in_a + span), bf16),
            pltpu.VMEM((head, in_b), bf16),
            pltpu.VMEM((in_a, tok), f32),
            pltpu.VMEM((in_b, tok), f32),
            pltpu.VMEM((in_a, wide), f32),
            pltpu.VMEM((in_b, wide), f32),
            pltpu.VMEM((in_a + span, wide), bf16),
            pltpu.VMEM((in_b, wide), bf16),
            pltpu.VMEM((in_b, wide), bf16),
            pltpu.VMEM((in_a, head), f32),
            pltpu.VMEM((in_a, head), f32),
            pltpu.VMEM((in_b, head), f32),
            pltpu.VMEM((in_b, head), f32),
            pltpu.VMEM((quads, tok, 4 * head), bf16),
            pltpu.VMEM((n, tok, cols), bf16),
            pltpu.VMEM((n // 2, tok, cols), bf16),
            pltpu.VMEM((n // 2, tok, cols), bf16),
            pltpu.VMEM((tok, cols), f32),
            pltpu.VMEM((tok, cols), bf16),
            dma((3, 2 * heads)),
            dma,
            dma,
            dma,
            dma((2, n)),
            dma((2, n)),
            dma((n,)),
            dma((n // 2,)),
            dma((n // 2,)),
            dma((quads,)),
            dma((quads,)),
            dma,
            dma,
        ],
        compiler_params=pltpu.CompilerParams(
            collective_id=0, has_side_effects=True, vmem_limit_bytes=(32 << 20) + n * (448 << 10)
        ),
    )(
        *[
            pltpu.with_memory_space_constraint(x, pltpu.HBM)
            for x in (queries, keys_values, output, dout, segment_ids)
        ],
        span_order,
    )
    last = lax.axis_index("section") == sections - 1
    return (
        jnp.where(last, jnp.zeros_like(dq), dq),
        jnp.where(last, jnp.zeros_like(dkv), dkv),
    )


def solution(mesh):
    rows = P("section", "ctx", None)
    return jax.shard_map(
        functools.partial(per_device, mesh.shape["section"], mesh.shape["ctx"]),
        mesh=mesh,
        in_specs=(rows, rows, rows, rows, P("section", "ctx"), P("ctx")),
        out_specs=(rows, rows),
        check_vma=False,
    )
```

```python
import functools

import jax
import jax.numpy as jnp
from jax import lax
from jax.experimental import pallas as pl
from jax.experimental.pallas import tpu as pltpu
from jax.sharding import PartitionSpec as P

MESH = pl.DeviceIdType.MESH
NEG = -1e30
DOT = functools.partial(lax.dot_general, preferred_element_type=jnp.float32)
NT = (((1,), (1,)), ((), ()))
NN = (((1,), (0,)), ((), ()))


def kernel(
    sections, n, head, heads,
    q_in, kv_in, o_in, d_in, seg_in, order_in,
    dq_out, dkv_out,
    q_s, o_s, d_s, kv_s, seg_s, meta_own, meta_s, flag_m, k_a, k_b, kt_a, kt_b, bias_a, bias_b,
    sc_a, sc_b, ds_a, p_a, ds_b, p_b, ds_be, ds_bl, dka_s, dva_s, dkb_s, dvb_s, dq_st, rs_st, rs_mid, rs_in, rs_own, kv_st,
    in_sem, own_sem, seg_sem, flag_sem, ag_send, ag_recv, rs_send, mid_recv, rs_recv, dq_send, dq_recv, kvo_send, kvo_recv,
):
    section = lax.axis_index("section")
    me = lax.axis_index("ctx")
    tok = kv_in.shape[1]
    span = tok // 2
    cols = 2 * head
    scale = head ** (-0.5)

    def loop(count, body):
        lax.fori_loop(0, count, lambda i, c: (body(i), c)[1], 0)

    chips = n // 2
    chip, core = me // 2, lax.rem(me, 2)
    partner = me + 1 - 2 * core

    def same(i):
        return 2 * lax.rem(chip + i + 1, chips) + core

    def other(i):
        return 2 * lax.rem(chip + i + 1, chips) + 1 - core

    quad = 4
    quads = heads // quad
    wide = quad * span

    def in_copies(i):
        g, half, h = i // (2 * quad), lax.rem(i // quad, 2), lax.rem(i, quad)
        at = pl.ds(pl.multiple_of((g * quad + h) * head, head), head)
        rows = pl.ds(pl.multiple_of(half * span, span), span)
        to = pl.ds(pl.multiple_of(h * span, span), span)
        return [
            pltpu.make_async_copy(src.at[0, rows, at], dst.at[g, half, to], in_sem.at[k, i])
            for k, (src, dst) in enumerate(((q_in, q_s), (d_in, d_s), (o_in, o_s)))
        ]

    own_kv = pltpu.make_async_copy(kv_in.at[0], kv_s.at[me], own_sem)
    own_kv.start()
    own_seg = pltpu.make_async_copy(seg_in, seg_s, seg_sem)
    own_seg.start()

    barrier = pltpu.get_barrier_semaphore()

    def greet(to):
        pl.semaphore_signal(barrier, inc=1, device_id={"ctx": to}, device_id_type=MESH)

    loop(chips - 1, lambda i: greet(same(i)))
    greet(partner)

    @pl.when(section > 0)
    def _():
        pl.semaphore_signal(barrier, inc=1, device_id={"section": section - 1}, device_id_type=MESH)

    @pl.when(section < sections - 1)
    def _():
        pl.semaphore_signal(barrier, inc=1, device_id={"section": section + 1}, device_id_type=MESH)


    lane = lax.broadcasted_iota(jnp.int32, (1, tok), 1)
    pos_row = jnp.where(lane < span, order_in[0] * span + lane, order_in[1] * span + lane - span)
    own_seg.wait()
    seg_row = seg_s[...]
    meta = jnp.concatenate([pos_row, seg_row, jnp.full((6, tok), order_in[0], jnp.int32)], axis=0)
    meta_own[...] = meta

    ends = (section == 0).astype(jnp.int32) + (section == sections - 1).astype(jnp.int32)
    pl.semaphore_wait(barrier, chips + 2 - ends)

    def ag_copies(to, slot, kv, info, via):
        return [
            pltpu.make_async_remote_copy(
                src, dst.at[slot], ag_send.at[k, via], ag_recv.at[k, slot],
                device_id={"ctx": to}, device_id_type=MESH,
            )
            for k, (src, dst) in enumerate(((info, meta_s), (kv, kv_s)))
        ]

    def ag_own(to):
        return ag_copies(to, me, kv_in.at[0], meta_own, to)

    def ag_relay(i):
        return ag_copies(partner, same(i), kv_s.at[same(i)], meta_s.at[same(i)], other(i))

    def start(copies):
        for c in copies:
            c.start()

    def arrived(frm):
        for c in ag_copies(partner, frm, kv_s.at[frm], meta_s.at[frm], frm):
            c.wait_recv()

    loop(chips - 1, lambda i: start(ag_own(same(i))))
    start(ag_own(partner))
    loop(2 * heads, lambda i: start(in_copies(i)))

    meta_s[me] = meta
    for acc in (dka_s, dva_s, dkb_s, dvb_s):
        acc[...] = jnp.zeros_like(acc)
    ds_a[(n + 1) * span :] = jnp.zeros((span, wide), jnp.bfloat16)
    kt_a[:, n * span :] = jnp.zeros((head, 2 * span), jnp.bfloat16)

    inside = jnp.where(lane < span, lane, lane - span)
    pos_e = (order_in[0] * span + inside).astype(jnp.float32)
    pos_l = (order_in[1] * span + inside).astype(jnp.float32)
    seg_f = seg_row.astype(jnp.float32)
    seg_r = pltpu.roll(seg_f, span, 1)
    seg_e = jnp.where(lane < span, seg_f, seg_r)
    seg_l = jnp.where(lane < span, seg_r, seg_f)

    def bias_of(key, pos, seg):
        ok = (key[:, 0:1] <= pos) & (key[:, 1:2] == seg)
        return jnp.where(ok, 0.0, NEG)

    def block(j):
        return pl.ds(pl.multiple_of(j * span, span), span)

    def flag_copy(j):
        return pltpu.make_async_copy(meta_s.at[j], flag_m.at[j], flag_sem.at[j])

    def prepare(j):
        flag_copy(j).start()
        got = meta_s[j]
        info = got.astype(jnp.float32).T
        kv = kv_s[j].astype(jnp.float32)
        flag = got[2:3] <= order_in[0]
        bias_a[block(j)] = bias_of(info[:span], pos_l, seg_l)
        k_a[block(j)] = kv_s[j, :span]
        kind = jnp.where(flag, 1.0, 0.0)
        lanes2 = jnp.concatenate([kind, kind], axis=1)
        kv_b = jnp.where(lanes2 > 0.5, kv[:span], kv[span:])
        k_b[block(j)] = kv_b.astype(jnp.bfloat16)
        info_b = jnp.where(kind[:, :8] > 0.5, info[:span], info[span:])
        bias_b[block(j)] = bias_of(
            info_b, jnp.where(flag, pos_e, pos_l), jnp.where(flag, seg_e, seg_l)
        )

        @pl.when(j == me)
        def _():
            last = pl.ds(n * span, span)
            k_a[last] = kv_s[j, span:]
            bias_a[last] = bias_of(info[span:], pos_l, seg_l)

    def turn(j):
        at = pl.ds(pl.multiple_of(j * tok, tok), tok)
        rows = pl.ds(pl.multiple_of(j * tok, tok), tok)
        kt_a[:, at] = k_a[rows, :head].astype(jnp.float32).T.astype(jnp.bfloat16)
        kt_b[:, at] = k_b[rows, :head].astype(jnp.float32).T.astype(jnp.bfloat16)

    own_kv.wait()
    prepare(me)

    kt_a[:, pl.ds(n * span, tok)] = jnp.concatenate(
        [k_a[pl.ds(n * span, span), :head].astype(jnp.float32).T, jnp.zeros((head, span), jnp.float32)],
        axis=1,
    ).astype(jnp.bfloat16)
    arrived(partner)
    prepare(partner)
    turn(chip)

    def relay(i):
        arrived(same(i))
        start(ag_relay(i))
        prepare(same(i))

    loop(chips - 1, relay)

    loop(2 * heads, lambda i: [c.wait() for c in in_copies(i)][0])

    def arrive(i):
        arrived(other(i))
        prepare(other(i))
        turn(other(i) // 2)

    loop(chips - 1, arrive)

    loop(n, lambda j: flag_copy(j).wait())

    def dq_copy(g):
        at = pl.ds(pl.multiple_of(g * quad * head, quad * head), quad * head)
        return pltpu.make_async_remote_copy(
            dq_st.at[g], dq_out.at[0, :, at], dq_send.at[g], dq_recv.at[g],
            device_id={"section": section - 1}, device_id_type=MESH,
        )

    size = max(d for d in range(1, 17) if (n + 1) % d == 0)
    steps = (n + 1) // size
    size *= span

    def each(count, init, body):
        return lax.fori_loop(0, count, body, init, unroll=count <= 8)

    def part(c):
        return pl.ds(pl.multiple_of(c * size, span), size)

    def twice(x):
        return jnp.concatenate([x, x], axis=1)

    def group(g):
        q_l, d_l = q_s[g, 1], d_s[g, 1]

        def delta_of(half):
            prod = d_s[g, half].astype(jnp.float32) * o_s[g, half].astype(jnp.float32)
            return jnp.sum(prod.T, axis=0, keepdims=True)

        delta_e, delta_l = delta_of(0), delta_of(1)

        def flag_of(j):
            return (flag_m[j, 2, 0] <= order_in[0]).astype(jnp.int32)

        def choose(f, early, late):
            return jnp.where(f > 0, early, late)

        low = jnp.full((1, wide), NEG, jnp.float32)
        none = jnp.zeros((1, wide), jnp.float32)

        def score_a(c, top):
            s = DOT(k_a[part(c), :head], q_l, NT) * scale + twice(bias_a[part(c)])
            sc_a[part(c)] = s
            return jnp.maximum(top, jnp.max(s, axis=0, keepdims=True))

        def score_b(j, tops):
            f = flag_of(j)
            s = DOT(k_b[block(j), :head], q_s[g, 1 - f], NT) * scale + twice(bias_b[block(j)])
            sc_b[block(j)] = s
            top = jnp.max(s, axis=0, keepdims=True)
            return (
                jnp.maximum(tops[0], choose(f, top, low)),
                jnp.maximum(tops[1], choose(f, low, top)),
            )

        top_e, top_l = each(n, (low, each(steps, low, score_a)), score_b)

        def exp_a(c, total):
            e = jnp.exp(sc_a[part(c)] - top_l)
            sc_a[part(c)] = e
            return total + jnp.sum(e, axis=0, keepdims=True)

        def exp_b(j, totals):
            f = flag_of(j)
            e = jnp.exp(sc_b[block(j)] - choose(f, top_e, top_l))
            sc_b[block(j)] = e
            total = jnp.sum(e, axis=0, keepdims=True)
            return (totals[0] + choose(f, total, none), totals[1] + choose(f, none, total))

        total_e, total_l = each(n, (none, each(steps, none, exp_a)), exp_b)
        inv_e, inv_l = 1.0 / total_e, 1.0 / total_l

        def grads_a(c, unused):
            p = sc_a[part(c)] * inv_l
            dp = DOT(k_a[part(c), head:], d_l, NT)
            ds = (p * (dp - delta_l)).astype(jnp.bfloat16)
            ds_a[part(c)] = ds
            p_a[part(c)] = p.astype(jnp.bfloat16)
            return unused

        def grads_b(j, unused):
            f = flag_of(j)
            p = sc_b[block(j)] * choose(f, inv_e, inv_l)
            dp = DOT(k_b[block(j), head:], d_s[g, 1 - f], NT)
            ds = p * (dp - choose(f, delta_e, delta_l))
            ds_e = ds * f.astype(jnp.float32)
            ds_be[block(j)] = ds_e.astype(jnp.bfloat16)
            ds_bl[block(j)] = (ds - ds_e).astype(jnp.bfloat16)
            ds_b[block(j)] = ds.astype(jnp.bfloat16)
            p_b[block(j)] = p.astype(jnp.bfloat16)
            return unused

        each(steps, 0, grads_a)
        each(n, 0, grads_b)
        dq_l = (DOT(kt_a[...], ds_a[...], NN) + DOT(kt_b[...], ds_bl[...], NN)) * scale
        dq_e = DOT(kt_b[...], ds_be[...], NN) * scale
        for half, dqt in ((0, dq_e), (1, dq_l)):
            dq = dqt.T.astype(jnp.bfloat16)
            dq_st[g, half * span : (half + 1) * span] = jnp.concatenate(
                [dq[h * span : (h + 1) * span] for h in range(quad)], axis=1
            )

        @pl.when(section > 0)
        def _():
            dq_copy(g).start()

        def terms_a(c, unused):
            dka_s[part(c)] += DOT(ds_a[part(c)], q_l, NN)
            dva_s[part(c)] += DOT(p_a[part(c)], d_l, NN)
            return unused

        def terms_b(j, unused):
            f = flag_of(j)
            dkb_s[block(j)] += DOT(ds_b[block(j)], q_s[g, 1 - f], NN)
            dvb_s[block(j)] += DOT(p_b[block(j)], d_s[g, 1 - f], NN)
            return unused

        each(steps, 0, terms_a)
        each(n, 0, terms_b)

    loop(quads, group)

    def terms(j):
        f = (flag_m[j, 2, 0] <= order_in[0]).astype(jnp.float32)
        dk_b, dv_b = dkb_s[block(j)], dvb_s[block(j)]
        dk_e, dv_e = dk_b * f, dv_b * f
        return jnp.concatenate(
            [
                jnp.concatenate([(dka_s[block(j)] + dk_e) * scale, dva_s[block(j)] + dv_e], axis=1),
                jnp.concatenate([(dk_b - dk_e) * scale, dv_b - dv_e], axis=1),
            ],
            axis=0,
        )

    def mid_copy(q):
        return pltpu.make_async_remote_copy(
            rs_st.at[2 * q + 1 - core], rs_mid.at[q], rs_send.at[2 * q + 1 - core], mid_recv.at[q],
            device_id={"ctx": partner}, device_id_type=MESH,
        )

    def rs_copy(to, slot):
        return pltpu.make_async_remote_copy(
            rs_st.at[to], rs_in.at[slot], rs_send.at[to], rs_recv.at[slot],
            device_id={"ctx": to}, device_id_type=MESH,
        )

    def hand(i):
        q = lax.rem(chip + i + 1, chips)
        rs_st[2 * q + 1 - core] = terms(2 * q + 1 - core).astype(jnp.bfloat16)
        mid_copy(q).start()

    loop(chips, hand)

    def scatter(i):
        to = same(i)
        mid_copy(to // 2).wait_recv()
        rs_st[to] = (terms(to) + rs_mid[to // 2].astype(jnp.float32)).astype(jnp.bfloat16)
        rs_copy(to, chip).start()

    loop(chips - 1, scatter)

    last = pl.ds(n * span, span)
    diag = jnp.concatenate([dka_s[last] * scale, dva_s[last]], axis=1)
    mid_copy(chip).wait_recv()
    own = terms(me) + jnp.concatenate([jnp.zeros_like(diag), diag], axis=0)
    rs_own[...] = own + rs_mid[chip].astype(jnp.float32)

    def gather(i):
        q = lax.rem(chip + i + 1, chips)
        rs_copy(same(i), q).wait_recv()
        rs_own[...] += rs_in[q].astype(jnp.float32)

    loop(chips - 1, gather)
    kv_st[...] = rs_own[...].astype(jnp.bfloat16)
    kvo = pltpu.make_async_remote_copy(
        kv_st, dkv_out.at[0], kvo_send, kvo_recv,
        device_id={"section": section - 1}, device_id_type=MESH,
    )

    @pl.when(section > 0)
    def _():
        kvo.start()

    def sent(copies):
        for c in copies:
            c.wait_send()

    def drain(i):
        sent(ag_own(same(i)))
        sent(ag_relay(i))
        rs_copy(same(i), chip).wait_send()

    loop(chips - 1, drain)
    sent(ag_own(partner))
    loop(chips, lambda q: mid_copy(q).wait_send())

    @pl.when(section > 0)
    def _():
        loop(quads, lambda g: dq_copy(g).wait_send())
        kvo.wait_send()

    @pl.when(section < sections - 1)
    def _():
        loop(quads, lambda g: dq_copy(g).wait_recv())
        kvo.wait_recv()


def per_device(sections, n, queries, keys_values, output, dout, segment_ids, span_order):
    head = keys_values.shape[2] // 2
    tok, width = queries.shape[1:]
    heads = width // head
    quads = heads // 4
    span = tok // 2
    wide = 4 * span
    cols = 2 * head
    in_a, in_b = (n + 1) * span, n * span
    any_spec = pl.BlockSpec(memory_space=pl.ANY)
    hbm_spec = pl.BlockSpec(memory_space=pltpu.HBM)
    f32, bf16, i32 = jnp.float32, jnp.bfloat16, jnp.int32
    dma = pltpu.SemaphoreType.DMA
    dq, dkv = pl.pallas_call(
        functools.partial(kernel, sections, n, head, heads),
        out_shape=(
            jax.ShapeDtypeStruct((1, tok, width), bf16),
            jax.ShapeDtypeStruct((1, tok, cols), bf16),
        ),
        in_specs=[hbm_spec] * 5 + [pl.BlockSpec(memory_space=pltpu.SMEM)],
        out_specs=(any_spec, any_spec),
        scratch_shapes=[
            pltpu.VMEM((quads, 2, wide, head), bf16),
            pltpu.VMEM((quads, 2, wide, head), bf16),
            pltpu.VMEM((quads, 2, wide, head), bf16),
            pltpu.VMEM((n, tok, cols), bf16),
            pltpu.VMEM((1, tok), i32),
            pltpu.VMEM((8, tok), i32),
            pltpu.VMEM((n, 8, tok), i32),
            pltpu.SMEM((n, 8, tok), i32),
            pltpu.VMEM((in_a, cols), bf16),
            pltpu.VMEM((in_b, cols), bf16),
            pltpu.VMEM((head, in_a + span), bf16),
            pltpu.VMEM((head, in_b), bf16),
            pltpu.VMEM((in_a, tok), f32),
            pltpu.VMEM((in_b, tok), f32),
            pltpu.VMEM((in_a, wide), f32),
            pltpu.VMEM((in_b, wide), f32),
            pltpu.VMEM((in_a + span, wide), bf16),
            pltpu.VMEM((in_a, wide), bf16),
            pltpu.VMEM((in_b, wide), bf16),
            pltpu.VMEM((in_b, wide), bf16),
            pltpu.VMEM((in_b, wide), bf16),
            pltpu.VMEM((in_b, wide), bf16),
            pltpu.VMEM((in_a, head), f32),
            pltpu.VMEM((in_a, head), f32),
            pltpu.VMEM((in_b, head), f32),
            pltpu.VMEM((in_b, head), f32),
            pltpu.VMEM((quads, tok, 4 * head), bf16),
            pltpu.VMEM((n, tok, cols), bf16),
            pltpu.VMEM((n // 2, tok, cols), bf16),
            pltpu.VMEM((n // 2, tok, cols), bf16),
            pltpu.VMEM((tok, cols), f32),
            pltpu.VMEM((tok, cols), bf16),
            dma((3, 2 * heads)),
            dma,
            dma,
            dma((n,)),
            dma((2, n)),
            dma((2, n)),
            dma((n,)),
            dma((n // 2,)),
            dma((n // 2,)),
            dma((quads,)),
            dma((quads,)),
            dma,
            dma,
        ],
        compiler_params=pltpu.CompilerParams(
            collective_id=0, has_side_effects=True, vmem_limit_bytes=(32 << 20) + n * (448 << 10)
        ),
    )(
        *[
            pltpu.with_memory_space_constraint(x, pltpu.HBM)
            for x in (queries, keys_values, output, dout, segment_ids)
        ],
        span_order,
    )
    last = lax.axis_index("section") == sections - 1
    return (
        jnp.where(last, jnp.zeros_like(dq), dq),
        jnp.where(last, jnp.zeros_like(dkv), dkv),
    )


def solution(mesh):
    rows = P("section", "ctx", None)
    return jax.shard_map(
        functools.partial(per_device, mesh.shape["section"], mesh.shape["ctx"]),
        mesh=mesh,
        in_specs=(rows, rows, rows, rows, P("section", "ctx"), P("ctx")),
        out_specs=(rows, rows),
        check_vma=False,
    )
```

```python
import functools

import jax
import jax.numpy as jnp
from jax import lax
from jax.experimental import pallas as pl
from jax.experimental.pallas import tpu as pltpu
from jax.sharding import PartitionSpec as P

MESH = pl.DeviceIdType.MESH
NEG = -1e30
DOT = functools.partial(lax.dot_general, preferred_element_type=jnp.float32)
NT = (((1,), (1,)), ((), ()))
NN = (((1,), (0,)), ((), ()))


def kernel(
    sections, n, head, heads,
    q_in, kv_in, o_in, d_in, seg_in, order_in,
    dq_out, dkv_out,
    q_s, o_s, d_s, kv_s, seg_s, meta_own, meta_s, flag_m, k_a, k_b, kt_a, kt_b, bias_a, bias_b,
    sc_a, sc_b, ds_a, p_a, ds_b, p_b, ds_be, ds_bl, dka_s, dva_s, dkb_s, dvb_s, dq_st, rs_st, rs_mid, rs_in, rs_own, kv_st,
    in_sem, own_sem, seg_sem, flag_sem, ag_send, ag_recv, rs_send, mid_recv, rs_recv, dq_send, dq_recv, kvo_send, kvo_recv,
):
    section = lax.axis_index("section")
    me = lax.axis_index("ctx")
    tok = kv_in.shape[1]
    span = tok // 2
    cols = 2 * head
    scale = head ** (-0.5)

    def loop(count, body):
        lax.fori_loop(0, count, lambda i, c: (body(i), c)[1], 0, unroll=count <= 4)

    chips = n // 2
    chip, core = me // 2, lax.rem(me, 2)
    partner = me + 1 - 2 * core

    def same(i):
        return 2 * lax.rem(chip + i + 1, chips) + core

    def other(i):
        return 2 * lax.rem(chip + i + 1, chips) + 1 - core

    quad = 4
    quads = heads // quad
    wide = quad * span

    def in_copies(i):
        g, half, h = i // (2 * quad), lax.rem(i // quad, 2), lax.rem(i, quad)
        at = pl.ds(pl.multiple_of((g * quad + h) * head, head), head)
        rows = pl.ds(pl.multiple_of(half * span, span), span)
        to = pl.ds(pl.multiple_of(h * span, span), span)
        return [
            pltpu.make_async_copy(src.at[0, rows, at], dst.at[g, half, to], in_sem.at[k, i])
            for k, (src, dst) in enumerate(((q_in, q_s), (d_in, d_s), (o_in, o_s)))
        ]

    own_kv = pltpu.make_async_copy(kv_in.at[0], kv_s.at[me], own_sem)
    own_kv.start()
    own_seg = pltpu.make_async_copy(seg_in, seg_s, seg_sem)
    own_seg.start()

    barrier = pltpu.get_barrier_semaphore()

    def greet(to):
        pl.semaphore_signal(barrier, inc=1, device_id={"ctx": to}, device_id_type=MESH)

    loop(chips - 1, lambda i: greet(same(i)))
    greet(partner)

    @pl.when(section > 0)
    def _():
        pl.semaphore_signal(barrier, inc=1, device_id={"section": section - 1}, device_id_type=MESH)

    @pl.when(section < sections - 1)
    def _():
        pl.semaphore_signal(barrier, inc=1, device_id={"section": section + 1}, device_id_type=MESH)


    lane = lax.broadcasted_iota(jnp.int32, (1, tok), 1)
    pos_row = jnp.where(lane < span, order_in[0] * span + lane, order_in[1] * span + lane - span)
    own_seg.wait()
    seg_row = seg_s[...]
    meta = jnp.concatenate([pos_row, seg_row, jnp.full((6, tok), order_in[0], jnp.int32)], axis=0)
    meta_own[...] = meta

    ends = (section == 0).astype(jnp.int32) + (section == sections - 1).astype(jnp.int32)
    pl.semaphore_wait(barrier, chips + 2 - ends)

    def ag_copies(to, slot, kv, info, via):
        return [
            pltpu.make_async_remote_copy(
                src, dst.at[slot], ag_send.at[k, via], ag_recv.at[k, slot],
                device_id={"ctx": to}, device_id_type=MESH,
            )
            for k, (src, dst) in enumerate(((info, meta_s), (kv, kv_s)))
        ]

    def ag_own(to):
        return ag_copies(to, me, kv_in.at[0], meta_own, to)

    def ag_relay(i):
        return ag_copies(partner, same(i), kv_s.at[same(i)], meta_s.at[same(i)], other(i))

    def start(copies):
        for c in copies:
            c.start()

    def arrived(frm):
        for c in ag_copies(partner, frm, kv_s.at[frm], meta_s.at[frm], frm):
            c.wait_recv()

    loop(chips - 1, lambda i: start(ag_own(same(i))))
    start(ag_own(partner))
    loop(2 * heads, lambda i: start(in_copies(i)))

    meta_s[me] = meta
    for acc in (dka_s, dva_s, dkb_s, dvb_s):
        acc[...] = jnp.zeros_like(acc)
    ds_a[(n + 1) * span :] = jnp.zeros((span, wide), jnp.bfloat16)
    kt_a[:, n * span :] = jnp.zeros((head, 2 * span), jnp.bfloat16)

    inside = jnp.where(lane < span, lane, lane - span)
    pos_e = (order_in[0] * span + inside).astype(jnp.float32)
    pos_l = (order_in[1] * span + inside).astype(jnp.float32)
    seg_f = seg_row.astype(jnp.float32)
    seg_r = pltpu.roll(seg_f, span, 1)
    seg_e = jnp.where(lane < span, seg_f, seg_r)
    seg_l = jnp.where(lane < span, seg_r, seg_f)

    def bias_of(key, pos, seg):
        ok = (key[:, 0:1] <= pos) & (key[:, 1:2] == seg)
        return jnp.where(ok, 0.0, NEG)

    def block(j):
        return pl.ds(pl.multiple_of(j * span, span), span)

    def flag_copy(j):
        return pltpu.make_async_copy(meta_s.at[j], flag_m.at[j], flag_sem.at[j])

    def prepare(j):
        flag_copy(j).start()
        got = meta_s[j]
        info = got.astype(jnp.float32).T
        kv = kv_s[j].astype(jnp.float32)
        flag = got[2:3] <= order_in[0]
        bias_a[block(j)] = bias_of(info[:span], pos_l, seg_l)
        k_a[block(j)] = kv_s[j, :span]
        kind = jnp.where(flag, 1.0, 0.0)
        lanes2 = jnp.concatenate([kind, kind], axis=1)
        kv_b = jnp.where(lanes2 > 0.5, kv[:span], kv[span:])
        k_b[block(j)] = kv_b.astype(jnp.bfloat16)
        info_b = jnp.where(kind[:, :8] > 0.5, info[:span], info[span:])
        bias_b[block(j)] = bias_of(
            info_b, jnp.where(flag, pos_e, pos_l), jnp.where(flag, seg_e, seg_l)
        )

        @pl.when(j == me)
        def _():
            last = pl.ds(n * span, span)
            k_a[last] = kv_s[j, span:]
            bias_a[last] = bias_of(info[span:], pos_l, seg_l)

    def turn(j):
        at = pl.ds(pl.multiple_of(j * tok, tok), tok)
        rows = pl.ds(pl.multiple_of(j * tok, tok), tok)
        kt_a[:, at] = k_a[rows, :head].astype(jnp.float32).T.astype(jnp.bfloat16)
        kt_b[:, at] = k_b[rows, :head].astype(jnp.float32).T.astype(jnp.bfloat16)

    own_kv.wait()
    prepare(me)

    kt_a[:, pl.ds(n * span, tok)] = jnp.concatenate(
        [k_a[pl.ds(n * span, span), :head].astype(jnp.float32).T, jnp.zeros((head, span), jnp.float32)],
        axis=1,
    ).astype(jnp.bfloat16)
    arrived(partner)
    prepare(partner)
    turn(chip)

    def relay(i):
        arrived(same(i))
        start(ag_relay(i))
        prepare(same(i))

    loop(chips - 1, relay)

    loop(2 * heads, lambda i: [c.wait() for c in in_copies(i)][0])

    def arrive(i):
        arrived(other(i))
        prepare(other(i))
        turn(other(i) // 2)

    loop(chips - 1, arrive)

    loop(n, lambda j: flag_copy(j).wait())

    def dq_copy(g):
        at = pl.ds(pl.multiple_of(g * quad * head, quad * head), quad * head)
        return pltpu.make_async_remote_copy(
            dq_st.at[g], dq_out.at[0, :, at], dq_send.at[g], dq_recv.at[g],
            device_id={"section": section - 1}, device_id_type=MESH,
        )

    size = max(d for d in range(1, 17) if (n + 1) % d == 0)
    steps = (n + 1) // size
    size *= span

    def each(count, init, body):
        return lax.fori_loop(0, count, body, init, unroll=count <= 8)

    def part(c):
        return pl.ds(pl.multiple_of(c * size, span), size)

    def twice(x):
        return jnp.concatenate([x, x], axis=1)

    def group(g):
        q_l, d_l = q_s[g, 1], d_s[g, 1]

        def delta_of(half):
            prod = d_s[g, half].astype(jnp.float32) * o_s[g, half].astype(jnp.float32)
            return jnp.sum(prod.T, axis=0, keepdims=True)

        delta_e, delta_l = delta_of(0), delta_of(1)

        def flag_of(j):
            return (flag_m[j, 2, 0] <= order_in[0]).astype(jnp.int32)

        def choose(f, early, late):
            return jnp.where(f > 0, early, late)

        low = jnp.full((1, wide), NEG, jnp.float32)
        none = jnp.zeros((1, wide), jnp.float32)

        def score_a(c, top):
            s = DOT(k_a[part(c), :head], q_l, NT) * scale + twice(bias_a[part(c)])
            sc_a[part(c)] = s
            return jnp.maximum(top, jnp.max(s, axis=0, keepdims=True))

        def score_b(j, tops):
            f = flag_of(j)
            s = DOT(k_b[block(j), :head], q_s[g, 1 - f], NT) * scale + twice(bias_b[block(j)])
            sc_b[block(j)] = s
            top = jnp.max(s, axis=0, keepdims=True)
            return (
                jnp.maximum(tops[0], choose(f, top, low)),
                jnp.maximum(tops[1], choose(f, low, top)),
            )

        top_e, top_l = each(n, (low, each(steps, low, score_a)), score_b)

        def exp_a(c, total):
            e = jnp.exp(sc_a[part(c)] - top_l)
            sc_a[part(c)] = e
            return total + jnp.sum(e, axis=0, keepdims=True)

        def exp_b(j, totals):
            f = flag_of(j)
            e = jnp.exp(sc_b[block(j)] - choose(f, top_e, top_l))
            sc_b[block(j)] = e
            total = jnp.sum(e, axis=0, keepdims=True)
            return (totals[0] + choose(f, total, none), totals[1] + choose(f, none, total))

        total_e, total_l = each(n, (none, each(steps, none, exp_a)), exp_b)
        inv_e, inv_l = 1.0 / total_e, 1.0 / total_l

        def grads_a(c, unused):
            p = sc_a[part(c)] * inv_l
            dp = DOT(k_a[part(c), head:], d_l, NT)
            ds = (p * (dp - delta_l)).astype(jnp.bfloat16)
            ds_a[part(c)] = ds
            p_a[part(c)] = p.astype(jnp.bfloat16)
            return unused

        def grads_b(j, unused):
            f = flag_of(j)
            p = sc_b[block(j)] * choose(f, inv_e, inv_l)
            dp = DOT(k_b[block(j), head:], d_s[g, 1 - f], NT)
            ds = p * (dp - choose(f, delta_e, delta_l))
            ds_e = ds * f.astype(jnp.float32)
            ds_be[block(j)] = ds_e.astype(jnp.bfloat16)
            ds_bl[block(j)] = (ds - ds_e).astype(jnp.bfloat16)
            ds_b[block(j)] = ds.astype(jnp.bfloat16)
            p_b[block(j)] = p.astype(jnp.bfloat16)
            return unused

        each(steps, 0, grads_a)
        each(n, 0, grads_b)
        dq_l = (DOT(kt_a[...], ds_a[...], NN) + DOT(kt_b[...], ds_bl[...], NN)) * scale
        dq_e = DOT(kt_b[...], ds_be[...], NN) * scale
        for half, dqt in ((0, dq_e), (1, dq_l)):
            dq = dqt.T.astype(jnp.bfloat16)
            dq_st[g, half * span : (half + 1) * span] = jnp.concatenate(
                [dq[h * span : (h + 1) * span] for h in range(quad)], axis=1
            )

        @pl.when(section > 0)
        def _():
            dq_copy(g).start()

        def terms_a(c, unused):
            dka_s[part(c)] += DOT(ds_a[part(c)], q_l, NN)
            dva_s[part(c)] += DOT(p_a[part(c)], d_l, NN)
            return unused

        def terms_b(j, unused):
            f = flag_of(j)
            dkb_s[block(j)] += DOT(ds_b[block(j)], q_s[g, 1 - f], NN)
            dvb_s[block(j)] += DOT(p_b[block(j)], d_s[g, 1 - f], NN)
            return unused

        each(steps, 0, terms_a)
        each(n, 0, terms_b)

    loop(quads, group)

    def terms(j):
        f = (flag_m[j, 2, 0] <= order_in[0]).astype(jnp.float32)
        dk_b, dv_b = dkb_s[block(j)], dvb_s[block(j)]
        dk_e, dv_e = dk_b * f, dv_b * f
        return jnp.concatenate(
            [
                jnp.concatenate([(dka_s[block(j)] + dk_e) * scale, dva_s[block(j)] + dv_e], axis=1),
                jnp.concatenate([(dk_b - dk_e) * scale, dv_b - dv_e], axis=1),
            ],
            axis=0,
        )

    def mid_copy(q):
        return pltpu.make_async_remote_copy(
            rs_st.at[2 * q + 1 - core], rs_mid.at[q], rs_send.at[2 * q + 1 - core], mid_recv.at[q],
            device_id={"ctx": partner}, device_id_type=MESH,
        )

    def rs_copy(to, slot):
        return pltpu.make_async_remote_copy(
            rs_st.at[to], rs_in.at[slot], rs_send.at[to], rs_recv.at[slot],
            device_id={"ctx": to}, device_id_type=MESH,
        )

    def hand(i):
        q = lax.rem(chip + i + 1, chips)
        rs_st[2 * q + 1 - core] = terms(2 * q + 1 - core).astype(jnp.bfloat16)
        mid_copy(q).start()

    loop(chips, hand)

    def scatter(i):
        to = same(i)
        mid_copy(to // 2).wait_recv()
        rs_st[to] = (terms(to) + rs_mid[to // 2].astype(jnp.float32)).astype(jnp.bfloat16)
        rs_copy(to, chip).start()

    loop(chips - 1, scatter)

    last = pl.ds(n * span, span)
    diag = jnp.concatenate([dka_s[last] * scale, dva_s[last]], axis=1)
    mid_copy(chip).wait_recv()
    own = terms(me) + jnp.concatenate([jnp.zeros_like(diag), diag], axis=0)
    rs_own[...] = own + rs_mid[chip].astype(jnp.float32)

    def gather(i):
        q = lax.rem(chip + i + 1, chips)
        rs_copy(same(i), q).wait_recv()
        rs_own[...] += rs_in[q].astype(jnp.float32)

    loop(chips - 1, gather)
    kv_st[...] = rs_own[...].astype(jnp.bfloat16)
    kvo = pltpu.make_async_remote_copy(
        kv_st, dkv_out.at[0], kvo_send, kvo_recv,
        device_id={"section": section - 1}, device_id_type=MESH,
    )

    @pl.when(section > 0)
    def _():
        kvo.start()

    def sent(copies):
        for c in copies:
            c.wait_send()

    def drain(i):
        sent(ag_own(same(i)))
        sent(ag_relay(i))
        rs_copy(same(i), chip).wait_send()

    loop(chips - 1, drain)
    sent(ag_own(partner))
    loop(chips, lambda q: mid_copy(q).wait_send())

    @pl.when(section > 0)
    def _():
        loop(quads, lambda g: dq_copy(g).wait_send())
        kvo.wait_send()

    @pl.when(section < sections - 1)
    def _():
        loop(quads, lambda g: dq_copy(g).wait_recv())
        kvo.wait_recv()


def per_device(sections, n, queries, keys_values, output, dout, segment_ids, span_order):
    head = keys_values.shape[2] // 2
    tok, width = queries.shape[1:]
    heads = width // head
    quads = heads // 4
    span = tok // 2
    wide = 4 * span
    cols = 2 * head
    in_a, in_b = (n + 1) * span, n * span
    any_spec = pl.BlockSpec(memory_space=pl.ANY)
    hbm_spec = pl.BlockSpec(memory_space=pltpu.HBM)
    f32, bf16, i32 = jnp.float32, jnp.bfloat16, jnp.int32
    dma = pltpu.SemaphoreType.DMA
    dq, dkv = pl.pallas_call(
        functools.partial(kernel, sections, n, head, heads),
        out_shape=(
            jax.ShapeDtypeStruct((1, tok, width), bf16),
            jax.ShapeDtypeStruct((1, tok, cols), bf16),
        ),
        in_specs=[hbm_spec] * 5 + [pl.BlockSpec(memory_space=pltpu.SMEM)],
        out_specs=(any_spec, any_spec),
        scratch_shapes=[
            pltpu.VMEM((quads, 2, wide, head), bf16),
            pltpu.VMEM((quads, 2, wide, head), bf16),
            pltpu.VMEM((quads, 2, wide, head), bf16),
            pltpu.VMEM((n, tok, cols), bf16),
            pltpu.VMEM((1, tok), i32),
            pltpu.VMEM((8, tok), i32),
            pltpu.VMEM((n, 8, tok), i32),
            pltpu.SMEM((n, 8, tok), i32),
            pltpu.VMEM((in_a, cols), bf16),
            pltpu.VMEM((in_b, cols), bf16),
            pltpu.VMEM((head, in_a + span), bf16),
            pltpu.VMEM((head, in_b), bf16),
            pltpu.VMEM((in_a, tok), f32),
            pltpu.VMEM((in_b, tok), f32),
            pltpu.VMEM((in_a, wide), f32),
            pltpu.VMEM((in_b, wide), f32),
            pltpu.VMEM((in_a + span, wide), bf16),
            pltpu.VMEM((in_a, wide), bf16),
            pltpu.VMEM((in_b, wide), bf16),
            pltpu.VMEM((in_b, wide), bf16),
            pltpu.VMEM((in_b, wide), bf16),
            pltpu.VMEM((in_b, wide), bf16),
            pltpu.VMEM((in_a, head), f32),
            pltpu.VMEM((in_a, head), f32),
            pltpu.VMEM((in_b, head), f32),
            pltpu.VMEM((in_b, head), f32),
            pltpu.VMEM((quads, tok, 4 * head), bf16),
            pltpu.VMEM((n, tok, cols), bf16),
            pltpu.VMEM((n // 2, tok, cols), bf16),
            pltpu.VMEM((n // 2, tok, cols), bf16),
            pltpu.VMEM((tok, cols), f32),
            pltpu.VMEM((tok, cols), bf16),
            dma((3, 2 * heads)),
            dma,
            dma,
            dma((n,)),
            dma((2, n)),
            dma((2, n)),
            dma((n,)),
            dma((n // 2,)),
            dma((n // 2,)),
            dma((quads,)),
            dma((quads,)),
            dma,
            dma,
        ],
        compiler_params=pltpu.CompilerParams(
            collective_id=0, has_side_effects=True, vmem_limit_bytes=(32 << 20) + n * (448 << 10)
        ),
    )(
        *[
            pltpu.with_memory_space_constraint(x, pltpu.HBM)
            for x in (queries, keys_values, output, dout, segment_ids)
        ],
        span_order,
    )
    last = lax.axis_index("section") == sections - 1
    return (
        jnp.where(last, jnp.zeros_like(dq), dq),
        jnp.where(last, jnp.zeros_like(dkv), dkv),
    )


def solution(mesh):
    rows = P("section", "ctx", None)
    return jax.shard_map(
        functools.partial(per_device, mesh.shape["section"], mesh.shape["ctx"]),
        mesh=mesh,
        in_specs=(rows, rows, rows, rows, P("section", "ctx"), P("ctx")),
        out_specs=(rows, rows),
        check_vma=False,
    )
```
